128 devices in a mesh: row: 32 (over z, x, core), col: 4 (over y).
Axes of the slice: x: 4, y: 4, z: 4, core: 2. Of those that a mesh axis runs over, the one named last changes fastest.
Arguments:
- pole_values: float32 [65536], P('row'), may hold values from 0.3 to 127.9, as said below
- rank_one: float32 [65536], P('row'), may hold values from -6 to 6
- deflated: int32 [65536], P('row'), may hold values 0 or 1
- onsite_energy: float32 [65536], P('row'), may hold values from 0.5 to 3
- secular_roots: float32 [16, 256], replicated, may hold values from 0 to 127.7, as said below
- column_order: int32 [16, 256], replicated, may hold values from 0 to 255, each once within a row
- q_blocks: bfloat16 [128, 512, 512], P('row'), may hold values from -1 to 1, as said below
- diag_blocks: float32 [128, 512, 512], P('row'), may hold values from -0.15625 to 0.15625
- coupling_blocks: float32 [128, 512, 512], P('row'), may hold values from -0.15625 to 0.15625
Outputs:
- refined_panel: float32 [16, 65536, 256], P(None, 'row', 'col')
- new_roots: float32 [16, 256], P(None, 'col')
The draws below stay inside these ranges and needn't reach their ends.
Inputs may be any that keep to these rules, and one draw needn't show every extreme that they name: `pole_values`: every pole lies 0.3 to 0.4 above a multiple of 0.5, at most 0.5 * 256 - 0.1. `secular_roots`: the root of index j in a panel lies between 0.5 j and 0.5 j + 0.2. `q_blocks`: each block is an orthogonal matrix rounded to bfloat16.
All inputs are finite; a program needn't handle non-finite values. No bound on the sum of `deflated` on one device may be relied on, other than what follows from the above.
Results may differ from the reference program's by a relative error of at most 0.0004.
The reference program's roundings to bfloat16 on the way (of `scaled` and `formed`) count: a program that leaves them out, or rounds other values in their place, can miss the bound.
Values may be sent and summed in bfloat16 or wider, within the bound.
No kernel may reach another device: no remote copies, remote signals or barrier semaphores. Data moves between devices by JAX's collectives and lax.ppermute only.
A program may use at most 192 MiB of HBM per device.

```python
import jax
import jax.numpy as jnp
from jax import lax

BLOCK = 512
PANEL = 256
PANELS = 16
NBLK = 128
N = 65536


def draw_pole_values(key, part):
    first_key, second_key = jax.random.split(jax.random.fold_in(key, 11))
    bins = jax.random.randint(first_key, (N,), 0, PANEL)
    offsets = jax.random.uniform(second_key, (N,), jnp.float32)
    return 0.5 * bins.astype(jnp.float32) + 0.3 + 0.1 * offsets


def draw_secular_roots(key, part):
    shifts = jax.random.uniform(jax.random.fold_in(key, 23), (PANELS, PANEL), jnp.float32)
    positions = jnp.arange(PANEL, dtype=jnp.float32)
    return 0.5 * positions[None, :] + 0.2 * shifts


def draw_q_blocks(key, part):
    gaussian = jax.random.normal(jax.random.fold_in(key, 37), (NBLK, BLOCK, BLOCK), jnp.float32)
    orthogonal, upper = jnp.linalg.qr(gaussian)
    return orthogonal.astype(jnp.bfloat16)


def touch_ends(drawn, key, low, largest):
    longest = drawn.shape.index(max(drawn.shape))
    spots = []
    for shift in (0, 1):
        where = [jax.random.randint(jax.random.fold_in(key, axis), (), 0, length) for axis, length in enumerate(drawn.shape)]
        where[longest] = (where[longest] + shift) % drawn.shape[longest]
        spots.append(tuple(where))
    return drawn.at[spots[0]].set(low).at[spots[1]].set(largest)


def shard_levels(key, dims, shards, smallest, largest):
    loudness = 1.0
    for axis_at, parts in shards:
        steps = jax.random.uniform(jax.random.fold_in(jax.random.fold_in(key, 6), axis_at), (parts,), jnp.float32, smallest / len(shards), largest / len(shards))
        loudness = loudness * jnp.repeat(jnp.exp(steps), dims[axis_at] // parts).reshape((-1,) + (1,) * (len(dims) - 1 - axis_at))
    return loudness


def scatter_about(own_key, extent, width, most, pieces=(), kind=jnp.bfloat16):
    loudness = shard_levels(own_key, extent, pieces, -0.22, 0.18) if pieces else 1.0
    entries = jax.random.normal(own_key, extent, jnp.float32) * width * loudness
    return jnp.minimum(jnp.maximum(entries, -most), most).astype(kind)


def setup_inputs(seed: int = 0) -> dict:
    key_of = jax.random.split(jax.random.key(seed), 10)
    pole_values = draw_pole_values(jax.random.fold_in(key_of[9], 71), 0)
    rank_one = scatter_about(key_of[1], (N,), 1.0, 6.0, ((0, 32),), jnp.float32)
    deflated = touch_ends((jax.random.randint(key_of[2], (N,), 0, 8) < 1).astype(jnp.int32), jax.random.fold_in(key_of[2], 1), 0, 1)
    onsite_energy = jnp.clip(0.5 + 2.5 * jax.random.uniform(key_of[3], (N,), jnp.float32) ** shard_levels(key_of[3], (N,), ((0, 32),), -0.2, 0.2), 0.5, 3.0)
    secular_roots = draw_secular_roots(jax.random.fold_in(key_of[9], 71), 0)
    column_order = jax.vmap(lambda own: jax.random.permutation(own, PANEL))(jax.random.split(key_of[5], PANELS)).reshape((PANELS, PANEL)).astype(jnp.int32)
    q_blocks = draw_q_blocks(jax.random.fold_in(key_of[9], 71), 0)
    diag_blocks = scatter_about(key_of[7], (NBLK, BLOCK, BLOCK), (3 * BLOCK) ** -0.5, 0.15625, ((0, 32),), jnp.float32)
    coupling_blocks = scatter_about(key_of[8], (NBLK, BLOCK, BLOCK), (3 * BLOCK) ** -0.5, 0.15625, ((0, 32),), jnp.float32)
    return dict(pole_values=pole_values, rank_one=rank_one, deflated=deflated, onsite_energy=onsite_energy, secular_roots=secular_roots, column_order=column_order, q_blocks=q_blocks, diag_blocks=diag_blocks, coupling_blocks=coupling_blocks)


EPSILON = 1e-06
HIGHEST = lax.Precision.HIGHEST

def reference(pole_values, rank_one, deflated, onsite_energy, secular_roots, column_order, q_blocks, diag_blocks, coupling_blocks):
    weights = rank_one * (1 - deflated).astype(jnp.float32)
    symmetric = 0.5 * (diag_blocks + jnp.swapaxes(diag_blocks, 1, 2))
    block_count = q_blocks.shape[0]
    block_size = q_blocks.shape[1]
    q_float = q_blocks.astype(jnp.float32)
    upper_blocks = jnp.concatenate([coupling_blocks[1:], jnp.zeros_like(coupling_blocks[:1])], axis=0)
    onsite_blocks = onsite_energy.reshape(block_count, block_size)

    def one_panel(inputs):
        roots_row, order_row = inputs
        chosen = roots_row[order_row]
        panel_size = chosen.shape[0]
        cauchy = weights[:, None] / (pole_values[:, None] - chosen[None, :])
        column_squares = lax.optimization_barrier(jnp.sum(cauchy * cauchy, axis=0))
        scaled = (cauchy * lax.rsqrt(column_squares + EPSILON)[None, :]).astype(jnp.bfloat16)
        blocked = scaled.astype(jnp.float32).reshape(block_count, block_size, panel_size)
        formed = jnp.einsum('bij,bjc->bic', q_float, blocked, precision=HIGHEST).astype(jnp.bfloat16)
        middle = formed.astype(jnp.float32)
        zero_block = jnp.zeros_like(middle[:1])
        lower_rows = jnp.concatenate([zero_block, middle[:-1]], axis=0)
        upper_rows = jnp.concatenate([middle[1:], zero_block], axis=0)
        operated = jnp.einsum('bij,bjc->bic', symmetric, middle, precision=HIGHEST)
        operated = operated + jnp.einsum('bij,bjc->bic', coupling_blocks, lower_rows, precision=HIGHEST)
        operated = operated + jnp.einsum('bji,bjc->bic', upper_blocks, upper_rows, precision=HIGHEST)
        operated = operated + onsite_blocks[:, :, None] * middle
        flat_rows = middle.reshape(-1, panel_size)
        flat_image = operated.reshape(-1, panel_size)
        gram = jnp.dot(flat_rows.T, flat_rows, precision=HIGHEST)
        projected = jnp.dot(flat_rows.T, flat_image, precision=HIGHEST)
        identity_mask = jnp.eye(panel_size, dtype=bool)
        residual = identity_mask.astype(jnp.float32) - gram
        spacing = chosen[None, :] - chosen[:, None] + identity_mask.astype(jnp.float32)
        update = jnp.where(identity_mask, 0.5 * residual, (projected + chosen[None, :] * residual) / spacing)
        updated = flat_rows + jnp.dot(flat_rows, update, precision=HIGHEST)
        column_sums = lax.optimization_barrier(jnp.sum(updated * updated, axis=0))
        refined = updated * jnp.sqrt(N / column_sums)[None, :]
        return (refined, jnp.diagonal(projected) / jnp.diagonal(gram))
    refined_panel, new_roots = lax.map(one_panel, (secular_roots, column_order))
    return (refined_panel, new_roots)
```

```python
import functools

import jax
import jax.numpy as jnp
from jax import lax
from jax.experimental import pallas as pl
from jax.experimental.pallas import tpu as pltpu
from jax.sharding import PartitionSpec as P

EPSILON = 1e-06
F32 = jnp.float32
BF16 = jnp.bfloat16
NT = (((1,), (1,)), ((), ()))
NN = (((1,), (0,)), ((), ()))
LANES = 128
MIB = 1 << 20


def dot(a, b, dims):
    return lax.dot_general(a, b, dims, preferred_element_type=F32)


def inverse(d):
    return 1.0 / d


def column_of(row):
    return jnp.transpose(jnp.broadcast_to(row, (LANES, row.shape[1])))


def row_of(column):
    return jnp.sum(jnp.transpose(column), axis=0, keepdims=True)


def joined(ref, p):
    return jnp.concatenate([ref[pl.ds(2 * p, 1), :], ref[pl.ds(2 * p + 1, 1), :]], axis=1)


def split(x):
    high = x.astype(BF16)
    return high, (x - high.astype(F32)).astype(BF16)


def squares_body(place, roots, order, poles, weights, chosen_out, squares_out, lam):
    panels, size = roots.shape
    rows = poles.shape[1]
    own = size // 4
    slots = lax.broadcasted_iota(jnp.int32, (size, size), 1)
    offset = place[0] * own

    def panel(p, carry):
        wanted = column_of(order[pl.ds(p, 1), :].astype(F32)).astype(jnp.int32)
        wanted = jnp.concatenate([wanted, wanted], axis=1)
        values = jnp.broadcast_to(roots[pl.ds(p, 1), :], (size, size))
        picked = jnp.sum(jnp.where(wanted == slots, values, 0.0), axis=1, keepdims=True)
        lam[...] = jnp.broadcast_to(picked, (size, LANES))
        parts = []
        for quarter in range(4):
            start = pl.multiple_of((offset + quarter * own) % size, own)
            here = lam[pl.ds(start, own), :]
            total = jnp.zeros((own, LANES), F32)
            for k in range(rows // LANES):
                lanes = pl.ds(k * LANES, LANES)
                term = weights[:, lanes] * inverse(poles[:, lanes] - here)
                total = total + term * term
            parts.append((here, total))
        for h in range(2):
            here, total = (jnp.concatenate(pair, axis=0) for pair in zip(*parts[2 * h : 2 * h + 2]))
            chosen_out[pl.ds(2 * p + h, 1), :] = jnp.transpose(here)[0:1]
            squares_out[pl.ds(2 * p + h, 1), :] = row_of(total)
        return carry

    lax.fori_loop(0, panels, panel, 0)


def form_body(
    place, chosen, squares, poles, weights, onsite, q, q_before, q_after,
    diag_hbm, coup_hbm, coup_after, formed, sent,
    edge, edge_formed, staged, operated, acc, factors, diag, coup, diagonals, sems,
):
    panels, size = formed.shape[:2]
    block = q.shape[1]
    count = q.shape[0]
    own = size // 4
    chunks = block // LANES
    core = place[1]
    load_diag = pltpu.make_async_copy(diag_hbm, diag, sems.at[0])
    load_coup = pltpu.make_async_copy(coup_hbm, coup, sems.at[1])
    load_diag.start()
    load_coup.start()

    def evaluate(lanes_at, lam, factor):
        lanes = pl.ds(lanes_at, LANES)
        cauchy = weights[:, lanes] * inverse(poles[:, lanes] - lam)
        return (cauchy * factor).astype(BF16)

    def panel(p, carry):
        lam = column_of(joined(chosen, p))
        factor = column_of(lax.rsqrt(joined(squares, p) + EPSILON))
        for b in range(count):
            for k in range(chunks):
                staged[b % 2, :, k * LANES : (k + 1) * LANES] = evaluate(
                    (b + 1) * block + k * LANES, lam, factor
                )
            made = dot(staged[b % 2], q[b], NT)
            formed[p, :, b * block : (b + 1) * block] = made.astype(BF16)
        for side, base in ((0, 0), (1, (count + 1) * block)):
            for k in range(chunks):
                edge[side, pl.ds(p * own, own), k * LANES : (k + 1) * LANES] = evaluate(
                    base + k * LANES, lam[:own], factor[:own]
                )
        return carry

    lax.fori_loop(0, panels, panel, 0)
    edge_formed[0] = dot(edge[0], q_before[...], NT).astype(BF16)
    edge_formed[1] = dot(edge[1], q_after[...], NT).astype(BF16)
    load_diag.wait()
    load_coup.wait()
    diagonals[...] = jnp.zeros(diagonals.shape, F32)

    def own_rows(b):
        if b < 0:
            return edge_formed[0]
        if b == count:
            return edge_formed[1]
        return formed[:, :own, b * block : (b + 1) * block].reshape(panels * own, block)

    for b in range(count):
        d = diag[b]
        terms = [(b, split(0.5 * (d + jnp.transpose(d))), NN), (b - 1, split(coup[b]), NT)]
        if b + 1 < count:
            terms.append((b + 1, split(coup[b + 1]), NN))
        else:
            terms.append((b + 1, (coup_after[...],), NN))
        for n, (source, pieces, dims) in enumerate(terms):
            left = own_rows(source)
            made = dot(left, pieces[0], dims)
            for piece in pieces[1:]:
                made = made + dot(left, piece, dims)
            acc[...] = made if n == 0 else acc[...] + made

        def finish(p, carry, b=b):
            at = pl.ds(p * own, own)
            lam = column_of(joined(chosen, p))[:own]
            g = diagonals[0, at, :]
            h = diagonals[1, at, :]
            for k in range(chunks):
                lanes = pl.ds(b * block + k * LANES, LANES)
                f = formed[p, :own, b * block + k * LANES : b * block + (k + 1) * LANES].astype(F32)
                o = acc[at, k * LANES : (k + 1) * LANES] + onsite[:, lanes] * f
                g = g + f * f
                h = h + f * o
                high, low = split(o - lam * f)
                operated[p, :own, lanes] = high
                operated[p, own:, lanes] = low
            diagonals[0, at, :] = g
            diagonals[1, at, :] = h
            return carry

        lax.fori_loop(0, panels, finish, 0)

    def project(p, carry):
        made = dot(operated[p], formed[p], NT)
        made = made[:own] + made[own:]
        at = pl.ds(p * own, own)
        both = jnp.concatenate([diagonals[0, at, :], diagonals[1, at, :]], axis=0)
        ends = jnp.broadcast_to(row_of(both), (8, LANES))
        rolled = pltpu.roll(ends, own, 1)
        line = lax.broadcasted_iota(jnp.int32, (8, LANES), 0)
        ends = jnp.where(line == 0, ends, rolled)
        half = own // 2
        for h in range(2):
            slot = h ^ core
            sent[slot, p, 0:half, :] = made[h * half : (h + 1) * half, :LANES]
            sent[slot, p, half : 2 * half, :] = made[h * half : (h + 1) * half, LANES:]
            sent[slot, p, 2 * half :, :] = ends
        return carry

    lax.fori_loop(0, panels, project, 0)


def update_body(place, arrived, chosen, sent):
    total = arrived[0]
    for n in range(1, arrived.shape[0]):
        total = total + arrived[n]
    p = place[2]
    half = (total.shape[0] - 8) // 2
    first = place[1] * half
    lam = joined(chosen, p)
    right = column_of(lam)
    right = jnp.where(place[1] == 0, right[:half], right[half : 2 * half])
    line = lax.broadcasted_iota(jnp.int32, (half, LANES), 0) + first
    lane = lax.broadcasted_iota(jnp.int32, (half, LANES), 1)
    same = line == lane
    spacing = right - lam[:, :LANES] + same.astype(F32)
    gram = total[2 * half : 2 * half + 1]
    proj = total[2 * half + 1 : 2 * half + 2]
    low = jnp.where(same, 1.0 + 0.5 * (1.0 - gram), total[:half] / spacing)
    high = total[half : 2 * half] / (right - lam[:, LANES:])
    lane = lax.broadcasted_iota(jnp.int32, (8, LANES), 1)
    inside = (lane >= first) & (lane < first + half)
    ends = jnp.where(inside, proj / jnp.where(inside, gram, 1.0), 0.0)
    made = jnp.concatenate([low, high, ends], axis=0)
    for n in range(sent.shape[0]):
        sent[n] = made


def refine_body(place, mine, other, formed, updated, sums, roots):
    panels, size = formed.shape[:2]
    own = size // 4
    half = own // 2
    zero = place[1] == 0

    def panel(p, carry):
        a, b = mine[p], other[p]
        low = jnp.where(zero, a, b)
        high = jnp.where(zero, b, a)
        u = jnp.concatenate(
            [
                jnp.concatenate([low[:half], low[half:own]], axis=1),
                jnp.concatenate([high[:half], high[half:own]], axis=1),
            ],
            axis=0,
        )
        made = dot(jnp.concatenate(split(u), axis=0), formed[p], NN)
        made = made[:own] + made[own:]
        updated[p] = made
        total = jnp.zeros((own, LANES), F32)
        for k in range(made.shape[1] // LANES):
            piece = made[:, k * LANES : (k + 1) * LANES]
            total = total + piece * piece
        sums[pl.ds(p, 1), :] = row_of(jnp.concatenate([total, jnp.zeros_like(total)], axis=0))
        roots[pl.ds(p, 1), :] = low[own : own + 1] + high[own : own + 1]
        return carry

    lax.fori_loop(0, panels, panel, 0)


def scale_body(sums, updated, refined, scaled, sems, *, order):
    panels, own, rows = updated.shape

    def copy(p):
        return pltpu.make_async_copy(scaled.at[p], refined.at[p], sems.at[p])

    def panel(p, carry):
        factor = column_of(jnp.sqrt(order / sums[pl.ds(p, 1), :]))[:own]
        for k in range(rows // LANES):
            lanes = slice(k * LANES, (k + 1) * LANES)
            scaled[p, :, lanes] = updated[p, :, lanes] * factor
        copy(p).start()
        return carry

    def wait(p, carry):
        copy(p).wait()
        return carry

    lax.fori_loop(0, panels, panel, 0)
    lax.fori_loop(0, panels, wait, 0)


def vmem():
    return pl.BlockSpec(memory_space=pltpu.VMEM)


def smem():
    return pl.BlockSpec(memory_space=pltpu.SMEM)


def hbm():
    return pl.BlockSpec(memory_space=pl.ANY)


def shards(
    pole_values, rank_one, deflated, onsite_energy, secular_roots, column_order,
    q_blocks, diag_blocks, coupling_blocks,
):
    rows = pole_values.shape[0]
    panels, size = secular_roots.shape
    count, block, _ = q_blocks.shape
    own = size // lax.axis_size("col")
    row_count = lax.axis_size("row")
    chips = row_count // 2
    row = lax.axis_index("row")
    place = jnp.stack([lax.axis_index("col"), row % 2, row // 2]).astype(jnp.int32)

    forward = [(i, (i + 1) % row_count) for i in range(row_count)]
    backward = [(i, (i - 1) % row_count) for i in range(row_count)]
    weights = rank_one * (1 - deflated).astype(F32)
    pair = jnp.stack([pole_values, weights])
    q_before = lax.ppermute(q_blocks[count - 1], "row", forward)
    after = lax.ppermute(
        jnp.concatenate([q_blocks[0], coupling_blocks[0].astype(BF16)], axis=0), "row", backward
    )
    pair_before = lax.ppermute(pair[:, rows - block :], "row", forward)
    pair_after = lax.ppermute(pair[:, :block], "row", backward)

    chosen, squares = pl.pallas_call(
        squares_body,
        out_shape=[jax.ShapeDtypeStruct((2 * panels, LANES), F32)] * 2,
        in_specs=[smem()] + [vmem()] * 4,
        out_specs=[vmem()] * 2,
        scratch_shapes=[pltpu.VMEM((size, LANES), F32)],
        compiler_params=pltpu.CompilerParams(vmem_limit_bytes=8 * MIB),
        name="squares",
    )(place, secular_roots, column_order, pole_values[None], weights[None])
    squares = over_rows(squares)

    poles_all = jnp.concatenate([pair_before[0], pole_values, pair_after[0]])[None]
    weights_all = jnp.concatenate(
        [
            jnp.where(row == 0, 0.0, pair_before[1]),
            weights,
            jnp.where(row == row_count - 1, 0.0, pair_after[1]),
        ]
    )[None]
    depth = own + 8
    formed, sent = pl.pallas_call(
        form_body,
        out_shape=[
            pltpu.VMEM((panels, size, rows), BF16),
            jax.ShapeDtypeStruct((2, panels, depth, LANES), F32),
        ],
        in_specs=[smem()] + [vmem()] * 8 + [hbm()] * 2 + [vmem()],
        out_specs=[vmem(), vmem()],
        scratch_shapes=[
            pltpu.VMEM((2, panels * own, block), BF16),
            pltpu.VMEM((2, panels * own, block), BF16),
            pltpu.VMEM((2, size, block), BF16),
            pltpu.VMEM((panels, 2 * own, rows), BF16),
            pltpu.VMEM((panels * own, block), F32),
            pltpu.VMEM((size, LANES), F32),
            pltpu.VMEM((count, block, block), F32),
            pltpu.VMEM((count, block, block), F32),
            pltpu.VMEM((2, panels * own, LANES), F32),
            pltpu.SemaphoreType.DMA((2,)),
        ],
        compiler_params=pltpu.CompilerParams(vmem_limit_bytes=38 * MIB),
        name="form",
    )(
        place, chosen, squares, poles_all, weights_all, onsite_energy[None], q_blocks,
        q_before, after[:block], diag_blocks, coupling_blocks, after[block:],
    )

    swap = [(i, i ^ 1) for i in range(row_count)]
    groups = [[c + 2 * k for k in range(chips)] for c in range(2)]
    spread = functools.partial(
        lax.all_to_all, axis_name="row", split_axis=0, concat_axis=0, tiled=True, axis_index_groups=groups
    )
    arrived = spread(sent[0] + lax.ppermute(sent[1], "row", swap))
    shares = pl.pallas_call(
        update_body,
        out_shape=jax.ShapeDtypeStruct((chips, depth, LANES), F32),
        in_specs=[smem()] + [vmem()] * 2,
        out_specs=vmem(),
        compiler_params=pltpu.CompilerParams(vmem_limit_bytes=8 * MIB),
        name="update",
    )(place, arrived, chosen)
    mine = spread(shares)
    other = lax.ppermute(mine, "row", swap)

    updated, sums, roots = pl.pallas_call(
        refine_body,
        out_shape=[
            pltpu.VMEM((panels, own, rows), F32),
            jax.ShapeDtypeStruct((panels, LANES), F32),
            jax.ShapeDtypeStruct((panels, LANES), F32),
        ],
        in_specs=[smem()] + [vmem()] * 3,
        out_specs=[vmem()] * 3,
        compiler_params=pltpu.CompilerParams(vmem_limit_bytes=12 * MIB),
        name="refine",
    )(place, mine, other, formed)
    refined = pl.pallas_call(
        functools.partial(scale_body, order=float(rows * row_count)),
        out_shape=jax.ShapeDtypeStruct((panels, own, rows), F32),
        in_specs=[vmem()] * 2,
        out_specs=hbm(),
        scratch_shapes=[
            pltpu.VMEM((panels, own, rows), F32),
            pltpu.SemaphoreType.DMA((panels,)),
        ],
        compiler_params=pltpu.CompilerParams(vmem_limit_bytes=12 * MIB),
        name="scale",
    )(over_rows(sums), updated)
    return jnp.transpose(refined, (0, 2, 1)), roots[:, :own]


def over_rows(value):
    def to(step):
        return [(i, step(i // 8, i // 2 % 4, i % 2)) for i in range(32)]

    value = value + lax.ppermute(value, "row", to(lambda z, x, c: z * 8 + x * 2 + 1 - c))
    for move in (
        lambda k: to(lambda z, x, c: z * 8 + (x + k) % 4 * 2 + c),
        lambda k: to(lambda z, x, c: (z + k) % 4 * 8 + x * 2 + c),
    ):
        value = value + sum([lax.ppermute(value, "row", move(k)) for k in (1, 2, 3)])
    return value


def solution(mesh):
    placed = (
        P("row"), P("row"), P("row"), P("row"), P(), P(),
        P("row", None, None), P("row", None, None), P("row", None, None),
    )
    return jax.shard_map(
        shards,
        mesh=mesh,
        in_specs=placed,
        out_specs=(P(None, "row", "col"), P(None, "col")),
        check_vma=False,
    )
```

```python
import functools

import jax
import jax.numpy as jnp
from jax import lax
from jax.experimental import pallas as pl
from jax.experimental.pallas import tpu as pltpu
from jax.sharding import PartitionSpec as P


EPSILON = 1e-06
F32 = jnp.float32
BF16 = jnp.bfloat16
NT = (((1,), (1,)), ((), ()))
NN = (((1,), (0,)), ((), ()))
LANES = 128
MIB = 1 << 20


def dot(a, b, dims):
    return lax.dot_general(a, b, dims, preferred_element_type=F32)


def inverse(d):
    return 1.0 / d


def column_of(row):
    return jnp.transpose(jnp.broadcast_to(row, (LANES, row.shape[1])))


def row_of(column):
    return jnp.sum(jnp.transpose(column), axis=0, keepdims=True)


def joined(ref, p):
    return jnp.concatenate([ref[pl.ds(2 * p, 1), :], ref[pl.ds(2 * p + 1, 1), :]], axis=1)


def split(x):
    high = x.astype(BF16)
    return high, (x - high.astype(F32)).astype(BF16)


def fetch(pairs, sems):
    copies = [pltpu.make_async_copy(src, dst, sems.at[n]) for n, (src, dst) in enumerate(pairs)]
    for copy in copies:
        copy.start()
    return copies


def squares_body(
    place, roots_hbm, order_hbm, poles_hbm, rank_hbm, deflated_hbm, chosen_out, columns_out, squares_out,
    roots, order, poles, rank, deflated, weights, picked, sems,
):
    panels, size = roots.shape
    rows = poles.shape[1]
    own = size // 4
    for copy in fetch(
        [(roots_hbm, roots), (order_hbm, order), (poles_hbm, poles), (rank_hbm, rank), (deflated_hbm, deflated)],
        sems,
    ):
        copy.wait()
    weights[...] = rank[...] * (1 - deflated[...]).astype(F32)
    slots = lax.broadcasted_iota(jnp.int32, (size, size), 1)
    offset = place[0] * own

    def pick(p, slot):
        wanted = column_of(order[pl.ds(p, 1), :].astype(F32)).astype(jnp.int32)
        wanted = jnp.concatenate([wanted, wanted], axis=1)
        values = jnp.broadcast_to(roots[pl.ds(p, 1), :], (size, size))
        value = jnp.sum(jnp.where(wanted == slots, values, 0.0), axis=1, keepdims=True)
        picked[slot] = jnp.broadcast_to(value, (size, LANES))

    def add_up(p, slot):
        parts = []
        for quarter in range(4):
            start = pl.multiple_of((offset + quarter * own) % size, own)
            here = picked[slot, pl.ds(start, own), :]
            columns_out[p, quarter * own : (quarter + 1) * own, :] = here
            total = jnp.zeros((own, LANES), F32)
            for k in range(rows // LANES):
                lanes = pl.ds(k * LANES, LANES)
                term = weights[:, lanes] * inverse(poles[:, lanes] - here)
                total = total + term * term
            parts.append((here, total))
        for h in range(2):
            here, total = (jnp.concatenate(pair, axis=0) for pair in zip(*parts[2 * h : 2 * h + 2]))
            chosen_out[pl.ds(2 * p + h, 1), :] = jnp.transpose(here)[0:1]
            squares_out[pl.ds(2 * p + h, 1), :] = row_of(total)

    def two(i, carry):
        pick(2 * i + 1, 1)
        add_up(2 * i, 0)
        pick(jnp.minimum(2 * i + 2, panels - 1), 0)
        add_up(2 * i + 1, 1)
        return carry

    pick(0, 0)
    lax.fori_loop(0, panels // 2, two, 0)


def form_body(
    place, columns, squares_a, squares_b, squares_c, squares_d, poles_hbm, rank_hbm, deflated_hbm, onsite_hbm,
    pair_before, pair_after, q_hbm, before_hbm, after_hbm, diag_hbm, coup_hbm,
    formed, kept, sent,
    staged, edge_formed, operated, acc, factors, squares, diag, coup, q, before, after, sym_parts, coup_parts,
    poles, rank, deflated, weights, onsite, grams, sems,
):
    panels, size = formed.shape[:2]
    count, block = q.shape[:2]
    own = size // 4
    chunks = block // LANES
    core = place[1]
    copies = fetch(
        [
            (poles_hbm, poles), (rank_hbm, rank), (deflated_hbm, deflated), (onsite_hbm, onsite),
            (q_hbm, q), (before_hbm, before), (after_hbm, after), (diag_hbm, diag), (coup_hbm, coup),
        ],
        sems,
    )
    squares[...] = squares_a[...] + squares_b[...] + squares_c[...] + squares_d[...]
    for copy in copies[:4]:
        copy.wait()
    weights[...] = rank[...] * (1 - deflated[...]).astype(F32)

    def prepare(p, slot):
        factors[slot] = column_of(lax.rsqrt(joined(squares, p) + EPSILON))

    def evaluate(p, slot):
        lam = columns[p]
        factor = factors[slot]
        for k in range(count * chunks):
            lanes = slice(k * LANES, (k + 1) * LANES)
            cauchy = weights[:, lanes] * inverse(poles[:, lanes] - lam)
            staged[slot, :, lanes] = (cauchy * factor).astype(BF16)
        for side, pair in enumerate((pair_before, pair_after)):
            for k in range(chunks):
                lanes = slice(k * LANES, (k + 1) * LANES)
                cauchy = pair[1:2, lanes] * inverse(pair[0:1, lanes] - lam[:own])
                operated[p, side * own : (side + 1) * own, lanes] = (cauchy * factor[:own]).astype(BF16)

    def multiply(p, slot):
        for b in range(count):
            lanes = slice(b * block, (b + 1) * block)
            formed[p, :, lanes] = dot(staged[slot, :, lanes], q[b], NT).astype(BF16)

    last = panels - 1

    def two(i, carry):
        p = 2 * i
        multiply(p, 0)
        evaluate(p + 1, 1)
        prepare(jnp.minimum(p + 2, last), 0)
        multiply(p + 1, 1)
        evaluate(jnp.minimum(p + 2, last), 0)
        prepare(jnp.minimum(p + 3, last), 1)
        return carry

    prepare(0, 0)
    prepare(1, 1)
    evaluate(0, 0)
    copies[4].wait()
    lax.fori_loop(0, panels // 2, two, 0)
    for copy in copies[5:]:
        copy.wait()
    for side, blocks in ((0, before[...]), (1, after[:block])):
        left = operated[:, side * own : (side + 1) * own, :block].reshape(panels * own, block)
        edge_formed[side] = dot(left, blocks, NT).astype(BF16)

    def own_rows(b):
        if b < 0:
            return edge_formed[0]
        if b == count:
            return edge_formed[1]
        return formed[:, :own, b * block : (b + 1) * block].reshape(panels * own, block)

    eye = lax.broadcasted_iota(jnp.int32, (LANES, LANES), 0) == lax.broadcasted_iota(jnp.int32, (LANES, LANES), 1)

    def ready_sym(b):
        for m in range(chunks):
            for n in range(m, chunks):
                at = slice(m * LANES, (m + 1) * LANES)
                to = slice(n * LANES, (n + 1) * LANES)
                value = 0.5 * (diag[b, at, to] + jnp.transpose(diag[b, to, at]))
                if m == n:
                    level = onsite[:, b * block + m * LANES : b * block + (m + 1) * LANES]
                    value = value + jnp.where(eye, level, 0.0)
                high, low = split(value)
                sym_parts[b % 2, 0, at, to] = high
                sym_parts[b % 2, 1, at, to] = low
                if m != n:
                    high, low = split(jnp.transpose(value))
                    sym_parts[b % 2, 0, to, at] = high
                    sym_parts[b % 2, 1, to, at] = low

    def ready_coup(b):
        high, low = split(coup[b])
        coup_parts[b, 0] = high
        coup_parts[b, 1] = low

    def apply(b):
        terms = [
            (own_rows(b), (sym_parts[b % 2, 0], sym_parts[b % 2, 1]), NN),
            (own_rows(b - 1), (coup_parts[b, 0], coup_parts[b, 1]), NT),
        ]
        if b + 1 < count:
            terms.append((own_rows(b + 1), (coup_parts[b + 1, 0], coup_parts[b + 1, 1]), NN))
        else:
            terms.append((own_rows(b + 1), (after[block:],), NN))
        made = None
        for left, pieces, dims in terms:
            for piece in pieces:
                term = dot(left, piece, dims)
                made = term if made is None else made + term
        acc[b % 2] = made

    def finish(b):
        for p in range(panels):
            at = slice(p * own, (p + 1) * own)
            lam = columns[p, :own]
            g = None if b == 0 else grams[at]
            for k in range(chunks):
                lanes = slice(b * block + k * LANES, b * block + (k + 1) * LANES)
                f = formed[p, :own, lanes].astype(F32)
                high, low = split(acc[b % 2, at, k * LANES : (k + 1) * LANES] - lam * f)
                g = f * f if g is None else g + f * f
                operated[p, :own, lanes] = high
                operated[p, own:, lanes] = low
            grams[at] = g

    ready_sym(0)
    ready_coup(0)
    ready_coup(1)
    for b in range(count):
        apply(b)
        if b + 1 < count:
            ready_sym(b + 1)
        if b + 2 < count:
            ready_coup(b + 2)
        if b > 0:
            finish(b - 1)
    finish(count - 1)

    half = own // 2

    def project(p):
        made = dot(operated[p], formed[p], NT)
        made = made[:own] + made[own:]
        g = grams[pl.ds(pl.multiple_of(p * own, own), own), :]
        ends = jnp.broadcast_to(row_of(jnp.concatenate([g, jnp.zeros_like(g)], axis=0)), (8, LANES))
        parts = [
            jnp.concatenate([made[h * half : (h + 1) * half, :LANES], made[h * half : (h + 1) * half, LANES:], ends], axis=0)
            for h in range(2)
        ]
        first = core == 0
        kept[p] = jnp.where(first, parts[0], parts[1])
        sent[p] = jnp.where(first, parts[1], parts[0])

    def project_two(i, carry):
        project(2 * i)
        project(2 * i + 1)
        return carry

    lax.fori_loop(0, panels // 2, project_two, 0)


def update_body(place, arrived, chosen, sent):
    total = arrived[0]
    for n in range(1, arrived.shape[0]):
        total = total + arrived[n]
    p = place[2]
    half = (total.shape[0] - 8) // 2
    first = place[1] * half
    lam = joined(chosen, p)
    right = column_of(lam)
    right = jnp.where(place[1] == 0, right[:half], right[half : 2 * half])
    line = lax.broadcasted_iota(jnp.int32, (half, LANES), 0) + first
    lane = lax.broadcasted_iota(jnp.int32, (half, LANES), 1)
    same = line == lane
    spacing = right - lam[:, :LANES] + same.astype(F32)
    gram = total[2 * half : 2 * half + 1]
    numerator = total[:half]
    low = jnp.where(same, 1.0 + 0.5 * (1.0 - gram), numerator / spacing)
    high = total[half : 2 * half] / (right - lam[:, LANES:])
    roots = jnp.where(same, numerator / jnp.where(same, gram, 1.0) + right, 0.0)
    ends = jnp.broadcast_to(jnp.sum(roots, axis=0, keepdims=True), (8, LANES))
    made = jnp.concatenate([low, high, ends], axis=0)
    for n in range(sent.shape[0]):
        sent[n] = made


def refine_body(place, mine, other, formed, updated, sums, roots):
    panels, size = formed.shape[:2]
    own = size // 4
    half = own // 2
    zero = place[1] == 0

    def panel(p):
        a, b = mine[p], other[p]
        low = jnp.where(zero, a, b)
        high = jnp.where(zero, b, a)
        u = jnp.concatenate(
            [
                jnp.concatenate([low[:half], low[half:own]], axis=1),
                jnp.concatenate([high[:half], high[half:own]], axis=1),
            ],
            axis=0,
        )
        made = dot(jnp.concatenate(split(u), axis=0), formed[p], NN)
        made = made[:own] + made[own:]
        updated[p] = made
        total = jnp.zeros((own, LANES), F32)
        for k in range(made.shape[1] // LANES):
            piece = made[:, k * LANES : (k + 1) * LANES]
            total = total + piece * piece
        sums[pl.ds(p, 1), :] = row_of(jnp.concatenate([total, jnp.zeros_like(total)], axis=0))
        roots[pl.ds(p, 1), :] = low[own : own + 1] + high[own : own + 1]

    def two(i, carry):
        panel(2 * i)
        panel(2 * i + 1)
        return carry

    lax.fori_loop(0, panels // 2, two, 0)


def scale_body(sums_a, sums_b, sums_c, sums_d, updated, refined, sums, scaled, sems, *, order):
    panels, own, rows = updated.shape
    sums[...] = sums_a[...] + sums_b[...] + sums_c[...] + sums_d[...]

    def copy(p):
        return pltpu.make_async_copy(scaled.at[p], refined.at[p], sems.at[p])

    def panel(p, carry):
        factor = column_of(jnp.sqrt(order / sums[pl.ds(p, 1), :]))[:own]
        for k in range(rows // LANES):
            lanes = slice(k * LANES, (k + 1) * LANES)
            scaled[p, :, lanes] = updated[p, :, lanes] * factor
        copy(p).start()
        return carry

    def wait(p, carry):
        copy(p).wait()
        return carry

    lax.fori_loop(0, panels, panel, 0)
    lax.fori_loop(0, panels, wait, 0)


def vmem():
    return pl.BlockSpec(memory_space=pltpu.VMEM)


def smem():
    return pl.BlockSpec(memory_space=pltpu.SMEM)


def hbm():
    return pl.BlockSpec(memory_space=pltpu.HBM)


def shards(
    pole_values, rank_one, deflated, onsite_energy, secular_roots, column_order,
    q_blocks, diag_blocks, coupling_blocks,
):
    rows = pole_values.shape[0]
    panels, size = secular_roots.shape
    count, block, _ = q_blocks.shape
    own = size // lax.axis_size("col")
    row_count = lax.axis_size("row")
    chips = row_count // 2
    row = lax.axis_index("row")
    place = jnp.stack([lax.axis_index("col"), row % 2, row // 2]).astype(jnp.int32)

    forward = [(i, (i + 1) % row_count) for i in range(row_count)]
    backward = [(i, (i - 1) % row_count) for i in range(row_count)]
    weights = rank_one * (1 - deflated).astype(F32)
    pair = jnp.stack([pole_values, weights])
    before = lax.ppermute(q_blocks[count - 1], "row", forward)
    after = lax.ppermute(
        jnp.concatenate([q_blocks[0], coupling_blocks[0].astype(BF16)], axis=0), "row", backward
    )
    ends = jnp.stack([row == 0, row == row_count - 1])
    pair_before = lax.ppermute(pair[:, rows - block :], "row", forward)
    pair_after = lax.ppermute(pair[:, :block], "row", backward)
    pair_before, pair_after = (
        jnp.stack([near[0], jnp.where(end, 0.0, near[1])])
        for near, end in ((pair_before, ends[0]), (pair_after, ends[1]))
    )
    vectors = (pole_values[None], rank_one[None], deflated[None])

    chosen, columns, squares = pl.pallas_call(
        squares_body,
        out_shape=[
            pltpu.VMEM((2 * panels, LANES), F32),
            pltpu.VMEM((panels, size, LANES), F32),
            pltpu.VMEM((2 * panels, LANES), F32),
        ],
        in_specs=[smem()] + [hbm()] * 5,
        out_specs=[vmem()] * 3,
        scratch_shapes=[
            pltpu.VMEM((panels, size), F32),
            pltpu.VMEM((panels, size), jnp.int32),
            pltpu.VMEM((1, rows), F32),
            pltpu.VMEM((1, rows), F32),
            pltpu.VMEM((1, rows), jnp.int32),
            pltpu.VMEM((1, rows), F32),
            pltpu.VMEM((2, size, LANES), F32),
            pltpu.SemaphoreType.DMA((5,)),
        ],
        compiler_params=pltpu.CompilerParams(vmem_limit_bytes=8 * MIB),
        name="squares",
    )(place, secular_roots, column_order, *vectors)

    depth = own + 8
    formed, kept, sent = pl.pallas_call(
        form_body,
        out_shape=[
            pltpu.VMEM((panels, size, rows), BF16),
            pltpu.VMEM((panels, depth, LANES), F32),
            pltpu.VMEM((panels, depth, LANES), F32),
        ],
        in_specs=[smem()] + [vmem()] * 5 + [hbm()] * 4 + [vmem()] * 2 + [hbm()] * 5,
        out_specs=[vmem()] * 3,
        scratch_shapes=[
            pltpu.VMEM((2, size, rows), BF16),
            pltpu.VMEM((2, panels * own, block), BF16),
            pltpu.VMEM((panels, 2 * own, rows), BF16),
            pltpu.VMEM((2, panels * own, block), F32),
            pltpu.VMEM((2, size, LANES), F32),
            pltpu.VMEM((2 * panels, LANES), F32),
            pltpu.VMEM((count, block, block), F32),
            pltpu.VMEM((count, block, block), F32),
            pltpu.VMEM((count, block, block), BF16),
            pltpu.VMEM((block, block), BF16),
            pltpu.VMEM((2 * block, block), BF16),
            pltpu.VMEM((2, 2, block, block), BF16),
            pltpu.VMEM((count, 2, block, block), BF16),
            pltpu.VMEM((1, rows), F32),
            pltpu.VMEM((1, rows), F32),
            pltpu.VMEM((1, rows), jnp.int32),
            pltpu.VMEM((1, rows), F32),
            pltpu.VMEM((1, rows), F32),
            pltpu.VMEM((panels * own, LANES), F32),
            pltpu.SemaphoreType.DMA((9,)),
        ],
        compiler_params=pltpu.CompilerParams(vmem_limit_bytes=42 * MIB),
        name="form",
    )(
        place, columns, *over_rows(squares), *vectors, onsite_energy[None], pair_before, pair_after,
        q_blocks, before, after, diag_blocks, coupling_blocks,
    )

    swap = [(i, i ^ 1) for i in range(row_count)]
    groups = [[c + 2 * k for k in range(chips)] for c in range(2)]
    spread = functools.partial(
        lax.all_to_all, axis_name="row", split_axis=0, concat_axis=0, tiled=True, axis_index_groups=groups
    )
    arrived = spread(kept + lax.ppermute(sent, "row", swap))
    shares = pl.pallas_call(
        update_body,
        out_shape=jax.ShapeDtypeStruct((chips, depth, LANES), F32),
        in_specs=[smem()] + [vmem()] * 2,
        out_specs=vmem(),
        compiler_params=pltpu.CompilerParams(vmem_limit_bytes=8 * MIB),
        name="update",
    )(place, arrived, chosen)
    mine = spread(shares)
    other = lax.ppermute(mine, "row", swap)

    updated, sums, roots = pl.pallas_call(
        refine_body,
        out_shape=[
            pltpu.VMEM((panels, own, rows), F32),
            pltpu.VMEM((panels, LANES), F32),
            jax.ShapeDtypeStruct((panels, LANES), F32),
        ],
        in_specs=[smem()] + [vmem()] * 3,
        out_specs=[vmem()] * 3,
        compiler_params=pltpu.CompilerParams(vmem_limit_bytes=12 * MIB),
        name="refine",
    )(place, mine, other, formed)
    refined = pl.pallas_call(
        functools.partial(scale_body, order=float(rows * row_count)),
        out_shape=jax.ShapeDtypeStruct((panels, own, rows), F32),
        in_specs=[vmem()] * 5,
        out_specs=hbm(),
        scratch_shapes=[
            pltpu.VMEM((panels, LANES), F32),
            pltpu.VMEM((panels, own, rows), F32),
            pltpu.SemaphoreType.DMA((panels,)),
        ],
        compiler_params=pltpu.CompilerParams(vmem_limit_bytes=12 * MIB),
        name="scale",
    )(*over_rows(sums), updated)
    return jnp.transpose(refined, (0, 2, 1)), roots[:, :own]


def over_rows(value):
    def to(step):
        return [(i, step(i // 8, i // 2 % 4, i % 2)) for i in range(32)]

    value = value + lax.ppermute(value, "row", to(lambda z, x, c: z * 8 + x * 2 + 1 - c))
    along_x = [to(lambda z, x, c, k=k: z * 8 + (x + k) % 4 * 2 + c) for k in (1, 2, 3)]
    value = value + sum([lax.ppermute(value, "row", move) for move in along_x])
    along_z = [to(lambda z, x, c, k=k: (z + k) % 4 * 8 + x * 2 + c) for k in (1, 2, 3)]
    return [value] + [lax.ppermute(value, "row", move) for move in along_z]


def solution(mesh):
    placed = (
        P("row"), P("row"), P("row"), P("row"), P(), P(),
        P("row", None, None), P("row", None, None), P("row", None, None),
    )
    return jax.shard_map(
        shards,
        mesh=mesh,
        in_specs=placed,
        out_specs=(P(None, "row", "col"), P(None, "col")),
        check_vma=False,
    )
```

```python
import functools

import jax
import jax.numpy as jnp
from jax import lax
from jax.experimental import pallas as pl
from jax.experimental.pallas import tpu as pltpu
from jax.sharding import PartitionSpec as P


EPSILON = 1e-06
F32 = jnp.float32
BF16 = jnp.bfloat16
NT = (((1,), (1,)), ((), ()))
NN = (((1,), (0,)), ((), ()))
LANES = 128
WIDE = 256
MIB = 1 << 20


def dot(a, b, dims):
    return lax.dot_general(a, b, dims, preferred_element_type=F32)


def inverse(d):
    return 1.0 / d


def column_of(row):
    return jnp.transpose(jnp.broadcast_to(row, (LANES, row.shape[1])))


def twice(column):
    return jnp.concatenate([column, column], axis=1)


def row_of(column):
    return jnp.sum(jnp.transpose(column), axis=0, keepdims=True)


def joined(ref, p):
    return jnp.concatenate([ref[pl.ds(2 * p, 1), :], ref[pl.ds(2 * p + 1, 1), :]], axis=1)


def split(x):
    high = x.astype(BF16)
    return high, (x - high.astype(F32)).astype(BF16)


def fetch(pairs, sems):
    copies = [pltpu.make_async_copy(src, dst, sems.at[n]) for n, (src, dst) in enumerate(pairs)]
    for copy in copies:
        copy.start()
    return copies


def squares_body(
    roots_hbm, order_hbm, poles_hbm, rank_hbm, deflated_hbm, chosen_out, squares_out,
    roots, order, poles, rank, deflated, weights, picked, sems,
):
    panels, size = roots.shape
    rows = poles.shape[1]
    own = size // 4
    for copy in fetch(
        [(roots_hbm, roots), (order_hbm, order), (poles_hbm, poles), (rank_hbm, rank), (deflated_hbm, deflated)],
        sems,
    ):
        copy.wait()
    weights[...] = rank[...] * (1 - deflated[...]).astype(F32)
    slots = lax.broadcasted_iota(jnp.int32, (size, size), 1)
    offset = lax.axis_index("col") * own

    def pick(p, slot):
        wanted = column_of(order[pl.ds(p, 1), :].astype(F32)).astype(jnp.int32)
        wanted = jnp.concatenate([wanted, wanted], axis=1)
        values = jnp.broadcast_to(roots[pl.ds(p, 1), :], (size, size))
        value = jnp.sum(jnp.where(wanted == slots, values, 0.0), axis=1, keepdims=True)
        picked[slot] = jnp.broadcast_to(value, (size, LANES))

    def add_up(p, slot):
        parts = []
        for quarter in range(4):
            start = pl.multiple_of((offset + quarter * own) % size, own)
            here = picked[slot, pl.ds(start, own), :]
            total = jnp.zeros((own, LANES), F32)
            for k in range(rows // LANES):
                lanes = pl.ds(k * LANES, LANES)
                term = weights[:, lanes] * inverse(poles[:, lanes] - here)
                total = total + term * term
            parts.append((here, total))
        for h in range(2):
            here, total = (jnp.concatenate(pair, axis=0) for pair in zip(*parts[2 * h : 2 * h + 2]))
            chosen_out[pl.ds(2 * p + h, 1), :] = jnp.transpose(here)[0:1]
            squares_out[pl.ds(2 * p + h, 1), :] = row_of(total)

    def two(i, carry):
        pick(2 * i + 1, 1)
        add_up(2 * i, 0)
        pick(jnp.minimum(2 * i + 2, panels - 1), 0)
        add_up(2 * i + 1, 1)
        return carry

    pick(0, 0)
    lax.fori_loop(0, panels // 2, two, 0)


def form_body(
    chosen, squares_a, squares_b, squares_c, squares_d, poles_hbm, rank_hbm, deflated_hbm, onsite_hbm,
    pair_before, pair_after, q_hbm, before_hbm, after_hbm, diag_hbm, coup_hbm,
    formed, kept, sent,
    staged, edge_formed, operated, acc, roots, own_roots, factors, squares, diag, coup, q, before, after, sym_parts, coup_parts,
    poles, rank, deflated, weights, onsite, grams, sems,
):
    panels, size = formed.shape[:2]
    count, block = q.shape[:2]
    own = size // 4
    chunks = block // LANES
    row = lax.axis_index("row")
    core = row % 2
    row_count = lax.axis_size("row")
    copies = fetch(
        [
            (poles_hbm, poles), (rank_hbm, rank), (deflated_hbm, deflated), (onsite_hbm, onsite),
            (q_hbm, q), (before_hbm, before), (after_hbm, after), (diag_hbm, diag), (coup_hbm, coup),
        ],
        sems,
    )
    squares[...] = squares_a[...] + squares_b[...] + squares_c[...] + squares_d[...]
    for copy in copies[:4]:
        copy.wait()
    weights[...] = rank[...] * (1 - deflated[...]).astype(F32)

    def prepare(p, slot):
        factors[slot] = column_of(lax.rsqrt(joined(squares, p) + EPSILON))
        lam = column_of(joined(chosen, p))
        roots[slot] = lam
        own_roots[p] = lam[:own]

    def evaluate(p, slot, b):
        lam = twice(roots[slot])
        factor = twice(factors[slot])
        for k in range(chunks // 2):
            lanes = slice(b * block + k * WIDE, b * block + (k + 1) * WIDE)
            cauchy = weights[:, lanes] * inverse(poles[:, lanes] - lam)
            staged[slot, :, lanes] = (cauchy * factor).astype(BF16)
        if b < 2:
            pair, missing = ((pair_before, row == 0), (pair_after, row == row_count - 1))[b]
            near = jnp.where(missing, 0.0, 1.0)
            for k in range(chunks // 2):
                lanes = slice(k * WIDE, (k + 1) * WIDE)
                cauchy = (near * pair[1:2, lanes]) * inverse(pair[0:1, lanes] - lam[:own])
                operated[p, b * own : (b + 1) * own, lanes] = (cauchy * factor[:own]).astype(BF16)

    def multiply(p, slot, b):
        lanes = slice(b * block, (b + 1) * block)
        formed[p, :, lanes] = dot(staged[slot, :, lanes], q[b], NT).astype(BF16)

    last = panels - 1

    def four(i, carry):
        for n in range(4):
            p = 4 * i + n
            for b in range(count):
                multiply(p, n % 2, b)
                evaluate(jnp.minimum(p + 1, last), 1 - n % 2, b)
            prepare(jnp.minimum(p + 2, last), n % 2)
        return carry

    prepare(0, 0)
    prepare(1, 1)
    for b in range(count):
        evaluate(0, 0, b)
    copies[4].wait()
    lax.fori_loop(0, panels // 4, four, 0)
    for copy in copies[5:]:
        copy.wait()
    for side, blocks in ((0, before[...]), (1, after[:block])):
        left = operated[:, side * own : (side + 1) * own, :block].reshape(panels * own, block)
        edge_formed[side] = dot(left, blocks, NT).astype(BF16)

    def own_rows(b):
        if b < 0:
            return edge_formed[0]
        if b == count:
            return edge_formed[1]
        return formed[:, :own, b * block : (b + 1) * block].reshape(panels * own, block)

    eye = lax.broadcasted_iota(jnp.int32, (LANES, LANES), 0) == lax.broadcasted_iota(jnp.int32, (LANES, LANES), 1)

    def ready_sym(b):
        for m in range(chunks):
            for n in range(m, chunks):
                at = slice(m * LANES, (m + 1) * LANES)
                to = slice(n * LANES, (n + 1) * LANES)
                value = 0.5 * (diag[b, at, to] + jnp.transpose(diag[b, to, at]))
                if m == n:
                    level = onsite[:, b * block + m * LANES : b * block + (m + 1) * LANES]
                    value = value + jnp.where(eye, level, 0.0)
                high, low = split(value)
                sym_parts[b % 2, 0, at, to] = high
                sym_parts[b % 2, 1, at, to] = low
                if m != n:
                    high, low = split(jnp.transpose(value))
                    sym_parts[b % 2, 0, to, at] = high
                    sym_parts[b % 2, 1, to, at] = low

    def ready_coup(b):
        high, low = split(coup[b])
        coup_parts[b, 0] = high
        coup_parts[b, 1] = low

    def apply(b):
        terms = [
            (own_rows(b), (sym_parts[b % 2, 0], sym_parts[b % 2, 1]), NN),
            (own_rows(b - 1), (coup_parts[b, 0], coup_parts[b, 1]), NT),
        ]
        if b + 1 < count:
            terms.append((own_rows(b + 1), (coup_parts[b + 1, 0], coup_parts[b + 1, 1]), NN))
        else:
            terms.append((own_rows(b + 1), (after[block:],), NN))
        made = None
        for left, pieces, dims in terms:
            for piece in pieces:
                term = dot(left, piece, dims)
                made = term if made is None else made + term
        acc[b % 2] = made

    def finish(b):
        for p in range(panels):
            at = slice(p * own, (p + 1) * own)
            lam = twice(own_roots[p])
            g = None if b == 0 else grams[at]
            for k in range(chunks // 2):
                lanes = slice(b * block + k * WIDE, b * block + (k + 1) * WIDE)
                f = formed[p, :own, lanes].astype(F32)
                high, low = split(acc[b % 2, at, k * WIDE : (k + 1) * WIDE] - lam * f)
                square = f * f
                square = square[:, :LANES] + square[:, LANES:]
                g = square if g is None else g + square
                operated[p, :own, lanes] = high
                operated[p, own:, lanes] = low
            grams[at] = g

    ready_sym(0)
    ready_coup(0)
    ready_coup(1)
    for b in range(count):
        apply(b)
        if b + 1 < count:
            ready_sym(b + 1)
        if b + 2 < count:
            ready_coup(b + 2)
        if b > 0:
            finish(b - 1)
    finish(count - 1)

    half = own // 2

    def project(p):
        made = dot(operated[p], formed[p], NT)
        made = made[:own] + made[own:]
        g = grams[pl.ds(pl.multiple_of(p * own, own), own), :]
        ends = jnp.broadcast_to(row_of(jnp.concatenate([g, jnp.zeros_like(g)], axis=0)), (8, LANES))
        parts = [
            jnp.concatenate([made[h * half : (h + 1) * half, :LANES], made[h * half : (h + 1) * half, LANES:], ends], axis=0)
            for h in range(2)
        ]
        first = core == 0
        kept[p] = jnp.where(first, parts[0], parts[1])
        sent[p] = jnp.where(first, parts[1], parts[0])

    def project_four(i, carry):
        for n in range(4):
            project(4 * i + n)
        return carry

    lax.fori_loop(0, panels // 4, project_four, 0)


def update_body(arrived, chosen, sent):
    total = arrived[0]
    for n in range(1, arrived.shape[0]):
        total = total + arrived[n]
    p = lax.axis_index("row") // 2
    core = lax.axis_index("row") % 2
    half = (total.shape[0] - 8) // 2
    first = core * half
    lam = joined(chosen, p)
    right = column_of(lam)
    right = jnp.where(core == 0, right[:half], right[half : 2 * half])
    line = lax.broadcasted_iota(jnp.int32, (half, LANES), 0) + first
    lane = lax.broadcasted_iota(jnp.int32, (half, LANES), 1)
    same = line == lane
    spacing = right - lam[:, :LANES] + same.astype(F32)
    gram = total[2 * half : 2 * half + 1]
    numerator = total[:half]
    low = jnp.where(same, 1.0 + 0.5 * (1.0 - gram), numerator / spacing)
    high = total[half : 2 * half] / (right - lam[:, LANES:])
    roots = jnp.where(same, numerator / jnp.where(same, gram, 1.0) + right, 0.0)
    ends = jnp.broadcast_to(jnp.sum(roots, axis=0, keepdims=True), (8, LANES))
    made = jnp.concatenate([low, high, ends], axis=0)
    for n in range(sent.shape[0]):
        sent[n] = made


def refine_body(mine, other, formed, updated, sums, roots):
    panels, size = formed.shape[:2]
    own = size // 4
    half = own // 2
    zero = lax.axis_index("row") % 2 == 0

    def panel(p):
        a, b = mine[p], other[p]
        low = jnp.where(zero, a, b)
        high = jnp.where(zero, b, a)
        u = jnp.concatenate(
            [
                jnp.concatenate([low[:half], low[half:own]], axis=1),
                jnp.concatenate([high[:half], high[half:own]], axis=1),
            ],
            axis=0,
        )
        made = dot(jnp.concatenate(split(u), axis=0), formed[p], NN)
        made = made[:own] + made[own:]
        updated[p] = made
        total = jnp.zeros((own, LANES), F32)
        for k in range(made.shape[1] // LANES):
            piece = made[:, k * LANES : (k + 1) * LANES]
            total = total + piece * piece
        sums[pl.ds(p, 1), :] = row_of(jnp.concatenate([total, jnp.zeros_like(total)], axis=0))
        roots[pl.ds(p, 1), :] = low[own : own + 1] + high[own : own + 1]

    def two(i, carry):
        panel(2 * i)
        panel(2 * i + 1)
        return carry

    lax.fori_loop(0, panels // 2, two, 0)


def scale_body(sums_a, sums_b, sums_c, sums_d, updated, refined, sums, scaled, sems, *, order):
    panels, own, rows = updated.shape
    sums[...] = sums_a[...] + sums_b[...] + sums_c[...] + sums_d[...]

    def copy(p):
        return pltpu.make_async_copy(scaled.at[p], refined.at[p], sems.at[p])

    def panel(p, carry):
        factor = column_of(jnp.sqrt(order / sums[pl.ds(p, 1), :]))[:own]
        for k in range(rows // LANES):
            lanes = slice(k * LANES, (k + 1) * LANES)
            scaled[p, :, lanes] = updated[p, :, lanes] * factor
        copy(p).start()
        return carry

    def wait(p, carry):
        copy(p).wait()
        return carry

    lax.fori_loop(0, panels, panel, 0)
    lax.fori_loop(0, panels, wait, 0)


def vmem():
    return pl.BlockSpec(memory_space=pltpu.VMEM)


def hbm():
    return pl.BlockSpec(memory_space=pltpu.HBM)


def anywhere():
    return pl.BlockSpec(memory_space=pl.ANY)


def shards(
    pole_values, rank_one, deflated, onsite_energy, secular_roots, column_order,
    q_blocks, diag_blocks, coupling_blocks,
):
    rows = pole_values.shape[0]
    panels, size = secular_roots.shape
    count, block, _ = q_blocks.shape
    own = size // lax.axis_size("col")
    row_count = lax.axis_size("row")
    chips = row_count // 2
    forward = [(i, (i + 1) % row_count) for i in range(row_count)]
    backward = [(i, (i - 1) % row_count) for i in range(row_count)]
    weights = rank_one * (1 - deflated).astype(F32)
    pair = jnp.stack([pole_values, weights])
    before = lax.ppermute(q_blocks[count - 1], "row", forward)
    after = lax.ppermute(
        jnp.concatenate([q_blocks[0], coupling_blocks[0].astype(BF16)], axis=0), "row", backward
    )
    pair_before = lax.ppermute(pair[:, rows - block :], "row", forward)
    pair_after = lax.ppermute(pair[:, :block], "row", backward)
    vectors = (pole_values[None], rank_one[None], deflated[None])

    chosen, squares = pl.pallas_call(
        squares_body,
        out_shape=[
            pltpu.VMEM((2 * panels, LANES), F32),
            pltpu.VMEM((2 * panels, LANES), F32),
        ],
        in_specs=[hbm()] * 5,
        out_specs=[vmem()] * 2,
        scratch_shapes=[
            pltpu.VMEM((panels, size), F32),
            pltpu.VMEM((panels, size), jnp.int32),
            pltpu.VMEM((1, rows), F32),
            pltpu.VMEM((1, rows), F32),
            pltpu.VMEM((1, rows), jnp.int32),
            pltpu.VMEM((1, rows), F32),
            pltpu.VMEM((2, size, LANES), F32),
            pltpu.SemaphoreType.DMA((5,)),
        ],
        compiler_params=pltpu.CompilerParams(vmem_limit_bytes=8 * MIB),
        name="squares",
    )(secular_roots, column_order, *vectors)

    depth = own + 8
    formed, kept, sent = pl.pallas_call(
        form_body,
        out_shape=[
            pltpu.VMEM((panels, size, rows), BF16),
            pltpu.VMEM((panels, depth, LANES), F32),
            pltpu.VMEM((panels, depth, LANES), F32),
        ],
        in_specs=[vmem()] * 5 + [hbm()] * 4 + [vmem()] * 2 + [hbm()] + [anywhere()] * 2 + [hbm()] * 2,
        out_specs=[vmem()] * 3,
        scratch_shapes=[
            pltpu.VMEM((2, size, rows), BF16),
            pltpu.VMEM((2, panels * own, block), BF16),
            pltpu.VMEM((panels, 2 * own, rows), BF16),
            pltpu.VMEM((2, panels * own, block), F32),
            pltpu.VMEM((2, size, LANES), F32),
            pltpu.VMEM((panels, own, LANES), F32),
            pltpu.VMEM((2, size, LANES), F32),
            pltpu.VMEM((2 * panels, LANES), F32),
            pltpu.VMEM((count, block, block), F32),
            pltpu.VMEM((count, block, block), F32),
            pltpu.VMEM((count, block, block), BF16),
            pltpu.VMEM((block, block), BF16),
            pltpu.VMEM((2 * block, block), BF16),
            pltpu.VMEM((2, 2, block, block), BF16),
            pltpu.VMEM((count, 2, block, block), BF16),
            pltpu.VMEM((1, rows), F32),
            pltpu.VMEM((1, rows), F32),
            pltpu.VMEM((1, rows), jnp.int32),
            pltpu.VMEM((1, rows), F32),
            pltpu.VMEM((1, rows), F32),
            pltpu.VMEM((panels * own, LANES), F32),
            pltpu.SemaphoreType.DMA((9,)),
        ],
        compiler_params=pltpu.CompilerParams(vmem_limit_bytes=38 * MIB),
        name="form",
    )(
        chosen, *over_rows(squares), *vectors, onsite_energy[None], pair_before, pair_after,
        q_blocks, before, after, diag_blocks, coupling_blocks,
    )

    swap = [(i, i ^ 1) for i in range(row_count)]
    groups = [[c + 2 * k for k in range(chips)] for c in range(2)]
    spread = functools.partial(
        lax.all_to_all, axis_name="row", split_axis=0, concat_axis=0, tiled=True, axis_index_groups=groups
    )
    arrived = spread(kept + lax.ppermute(sent, "row", swap))
    shares = pl.pallas_call(
        update_body,
        out_shape=jax.ShapeDtypeStruct((chips, depth, LANES), F32),
        in_specs=[vmem()] * 2,
        out_specs=vmem(),
        compiler_params=pltpu.CompilerParams(vmem_limit_bytes=8 * MIB),
        name="update",
    )(arrived, chosen)
    mine = spread(shares)
    other = lax.ppermute(mine, "row", swap)

    updated, sums, roots = pl.pallas_call(
        refine_body,
        out_shape=[
            pltpu.VMEM((panels, own, rows), F32),
            pltpu.VMEM((panels, LANES), F32),
            jax.ShapeDtypeStruct((panels, LANES), F32),
        ],
        in_specs=[vmem()] * 3,
        out_specs=[vmem()] * 3,
        compiler_params=pltpu.CompilerParams(vmem_limit_bytes=12 * MIB),
        name="refine",
    )(mine, other, formed)
    refined = pl.pallas_call(
        functools.partial(scale_body, order=float(rows * row_count)),
        out_shape=jax.ShapeDtypeStruct((panels, own, rows), F32),
        in_specs=[vmem()] * 5,
        out_specs=hbm(),
        scratch_shapes=[
            pltpu.VMEM((panels, LANES), F32),
            pltpu.VMEM((panels, own, rows), F32),
            pltpu.SemaphoreType.DMA((panels,)),
        ],
        compiler_params=pltpu.CompilerParams(vmem_limit_bytes=12 * MIB),
        name="scale",
    )(*over_rows(sums), updated)
    return jnp.transpose(refined, (0, 2, 1)), roots[:, :own]


def over_rows(value):
    def to(step):
        return [(i, step(i // 8, i // 2 % 4, i % 2)) for i in range(32)]

    value = value + lax.ppermute(value, "row", to(lambda z, x, c: z * 8 + x * 2 + 1 - c))
    along_x = [to(lambda z, x, c, k=k: z * 8 + (x + k) % 4 * 2 + c) for k in (1, 2, 3)]
    value = value + sum([lax.ppermute(value, "row", move) for move in along_x])
    along_z = [to(lambda z, x, c, k=k: (z + k) % 4 * 8 + x * 2 + c) for k in (1, 2, 3)]
    return [value] + [lax.ppermute(value, "row", move) for move in along_z]


def solution(mesh):
    placed = (
        P("row"), P("row"), P("row"), P("row"), P(), P(),
        P("row", None, None), P("row", None, None), P("row", None, None),
    )
    return jax.shard_map(
        shards,
        mesh=mesh,
        in_specs=placed,
        out_specs=(P(None, "row", "col"), P(None, "col")),
        check_vma=False,
    )
```

```python
import functools

import jax
import jax.numpy as jnp
from jax import lax
from jax.experimental import pallas as pl
from jax.experimental.pallas import tpu as pltpu
from jax.sharding import PartitionSpec as P


EPSILON = 1e-06
F32 = jnp.float32
BF16 = jnp.bfloat16
NT = (((1,), (1,)), ((), ()))
NN = (((1,), (0,)), ((), ()))
LANES = 128
WIDE = 256
MIB = 1 << 20


def dot(a, b, dims):
    return lax.dot_general(a, b, dims, preferred_element_type=F32)


def inverse(d):
    return 1.0 / d


def column_of(row):
    return jnp.transpose(jnp.broadcast_to(row, (LANES, row.shape[1])))


def twice(column):
    return jnp.concatenate([column, column], axis=1)


def row_of(column):
    return jnp.sum(jnp.transpose(column), axis=0, keepdims=True)


def joined(ref, p):
    return jnp.concatenate([ref[pl.ds(2 * p, 1), :], ref[pl.ds(2 * p + 1, 1), :]], axis=1)


def split(x):
    high = x.astype(BF16)
    return high, (x - high.astype(F32)).astype(BF16)


def fetch(pairs, sems):
    copies = [pltpu.make_async_copy(src, dst, sems.at[n]) for n, (src, dst) in enumerate(pairs)]
    for copy in copies:
        copy.start()
    return copies


def squares_body(
    roots_hbm, order_hbm, poles_hbm, rank_hbm, deflated_hbm, chosen_out, squares_out,
    roots, order, poles, rank, deflated, weights, picked, sems,
):
    panels, size = roots.shape
    rows = poles.shape[1]
    own = size // 4
    for copy in fetch(
        [(roots_hbm, roots), (order_hbm, order), (poles_hbm, poles), (rank_hbm, rank), (deflated_hbm, deflated)],
        sems,
    ):
        copy.wait()
    weights[...] = rank[...] * (1 - deflated[...]).astype(F32)
    slots = lax.broadcasted_iota(jnp.int32, (size, size), 1)
    offset = lax.axis_index("col") * own

    def pick(p, slot):
        wanted = column_of(order[pl.ds(p, 1), :].astype(F32)).astype(jnp.int32)
        wanted = jnp.concatenate([wanted, wanted], axis=1)
        values = jnp.broadcast_to(roots[pl.ds(p, 1), :], (size, size))
        value = jnp.sum(jnp.where(wanted == slots, values, 0.0), axis=1, keepdims=True)
        picked[slot] = jnp.broadcast_to(value, (size, LANES))

    def add_up(p, slot):
        parts = []
        for quarter in range(4):
            start = pl.multiple_of((offset + quarter * own) % size, own)
            here = picked[slot, pl.ds(start, own), :]
            total = jnp.zeros((own, LANES), F32)
            for k in range(rows // LANES):
                lanes = pl.ds(k * LANES, LANES)
                term = weights[:, lanes] * inverse(poles[:, lanes] - here)
                total = total + term * term
            parts.append((here, total))
        for h in range(2):
            here, total = (jnp.concatenate(pair, axis=0) for pair in zip(*parts[2 * h : 2 * h + 2]))
            chosen_out[pl.ds(2 * p + h, 1), :] = jnp.transpose(here)[0:1]
            squares_out[pl.ds(2 * p + h, 1), :] = row_of(total)

    def four(i, carry):
        for n in range(4):
            pick(jnp.minimum(4 * i + n + 1, panels - 1), 1 - n % 2)
            add_up(4 * i + n, n % 2)
        return carry

    pick(0, 0)
    lax.fori_loop(0, panels // 4, four, 0)


def form_body(
    chosen, squares_a, squares_b, squares_c, squares_d, poles_hbm, rank_hbm, deflated_hbm, onsite_hbm,
    pair_before, pair_after, q_hbm, before_hbm, after_hbm, diag_hbm, coup_hbm,
    formed, kept, sent,
    staged, edge_formed, operated, acc, roots, own_roots, factors, squares, diag, coup, q, before, after, sym_parts, coup_parts,
    poles, rank, deflated, weights, onsite, grams, sems,
):
    panels, size = formed.shape[:2]
    count, block = q.shape[:2]
    own = size // 4
    chunks = block // LANES
    row = lax.axis_index("row")
    core = row % 2
    row_count = lax.axis_size("row")
    copies = fetch(
        [
            (poles_hbm, poles), (rank_hbm, rank), (deflated_hbm, deflated), (onsite_hbm, onsite),
            (q_hbm, q), (before_hbm, before), (after_hbm, after), (diag_hbm, diag), (coup_hbm, coup),
        ],
        sems,
    )
    squares[...] = squares_a[...] + squares_b[...] + squares_c[...] + squares_d[...]
    for copy in copies[:4]:
        copy.wait()
    weights[...] = rank[...] * (1 - deflated[...]).astype(F32)

    def prepare(p, slot):
        factors[slot] = column_of(lax.rsqrt(joined(squares, p) + EPSILON))
        lam = column_of(joined(chosen, p))
        roots[slot] = lam
        own_roots[p] = lam[:own]

    def evaluate(p, slot, b):
        lam = twice(roots[slot])
        factor = twice(factors[slot])
        for k in range(chunks // 2):
            lanes = slice(b * block + k * WIDE, b * block + (k + 1) * WIDE)
            cauchy = weights[:, lanes] * inverse(poles[:, lanes] - lam)
            staged[slot, :, lanes] = (cauchy * factor).astype(BF16)
        if b < 2:
            pair, missing = ((pair_before, row == 0), (pair_after, row == row_count - 1))[b]
            near = jnp.where(missing, 0.0, 1.0)
            for k in range(chunks // 2):
                lanes = slice(k * WIDE, (k + 1) * WIDE)
                cauchy = (near * pair[1:2, lanes]) * inverse(pair[0:1, lanes] - lam[:own])
                operated[p, b * own : (b + 1) * own, lanes] = (cauchy * factor[:own]).astype(BF16)

    def multiply(p, slot, b):
        lanes = slice(b * block, (b + 1) * block)
        formed[p, :, lanes] = dot(staged[slot, :, lanes], q[b], NT).astype(BF16)

    last = panels - 1

    def four(i, carry):
        for n in range(4):
            p = 4 * i + n
            for b in range(count):
                multiply(p, n % 2, b)
                evaluate(jnp.minimum(p + 1, last), 1 - n % 2, b)
            prepare(jnp.minimum(p + 2, last), n % 2)
        return carry

    prepare(0, 0)
    prepare(1, 1)
    for b in range(count):
        evaluate(0, 0, b)
    copies[4].wait()
    lax.fori_loop(0, panels // 4, four, 0)
    for copy in copies[5:]:
        copy.wait()
    for side, blocks in ((0, before[...]), (1, after[:block])):
        left = operated[:, side * own : (side + 1) * own, :block].reshape(panels * own, block)
        edge_formed[side] = dot(left, blocks, NT).astype(BF16)

    def own_rows(b):
        if b < 0:
            return edge_formed[0]
        if b == count:
            return edge_formed[1]
        return formed[:, :own, b * block : (b + 1) * block].reshape(panels * own, block)

    eye = lax.broadcasted_iota(jnp.int32, (LANES, LANES), 0) == lax.broadcasted_iota(jnp.int32, (LANES, LANES), 1)

    def ready_sym(b):
        for m in range(chunks):
            for n in range(m, chunks):
                at = slice(m * LANES, (m + 1) * LANES)
                to = slice(n * LANES, (n + 1) * LANES)
                value = 0.5 * (diag[b, at, to] + jnp.transpose(diag[b, to, at]))
                if m == n:
                    level = onsite[:, b * block + m * LANES : b * block + (m + 1) * LANES]
                    value = value + jnp.where(eye, level, 0.0)
                high, low = split(value)
                sym_parts[b % 2, 0, at, to] = high
                sym_parts[b % 2, 1, at, to] = low
                if m != n:
                    high, low = split(jnp.transpose(value))
                    sym_parts[b % 2, 0, to, at] = high
                    sym_parts[b % 2, 1, to, at] = low

    def ready_coup(b):
        high, low = split(coup[b])
        coup_parts[b, 0] = high
        coup_parts[b, 1] = low

    def apply(b):
        terms = [
            (own_rows(b), (sym_parts[b % 2, 0], sym_parts[b % 2, 1]), NN),
            (own_rows(b - 1), (coup_parts[b, 0], coup_parts[b, 1]), NT),
        ]
        if b + 1 < count:
            terms.append((own_rows(b + 1), (coup_parts[b + 1, 0], coup_parts[b + 1, 1]), NN))
        else:
            terms.append((own_rows(b + 1), (after[block:],), NN))
        made = None
        for left, pieces, dims in terms:
            for piece in pieces:
                term = dot(left, piece, dims)
                made = term if made is None else made + term
        acc[b % 2] = made

    def finish(b):
        for p in range(panels):
            at = slice(p * own, (p + 1) * own)
            lam = twice(own_roots[p])
            g = None if b == 0 else grams[at]
            for k in range(chunks // 2):
                lanes = slice(b * block + k * WIDE, b * block + (k + 1) * WIDE)
                f = formed[p, :own, lanes].astype(F32)
                high, low = split(acc[b % 2, at, k * WIDE : (k + 1) * WIDE] - lam * f)
                square = f * f
                square = square[:, :LANES] + square[:, LANES:]
                g = square if g is None else g + square
                operated[p, :own, lanes] = high
                operated[p, own:, lanes] = low
            grams[at] = g

    ready_sym(0)
    ready_coup(0)
    ready_coup(1)
    for b in range(count):
        apply(b)
        if b + 1 < count:
            ready_sym(b + 1)
        if b + 2 < count:
            ready_coup(b + 2)
        if b > 0:
            finish(b - 1)
    finish(count - 1)

    half = own // 2

    def project(p):
        made = dot(operated[p], formed[p], NT)
        made = made[:own] + made[own:]
        g = grams[pl.ds(pl.multiple_of(p * own, own), own), :]
        ends = jnp.broadcast_to(row_of(jnp.concatenate([g, jnp.zeros_like(g)], axis=0)), (8, LANES))
        parts = [
            jnp.concatenate([made[h * half : (h + 1) * half, :LANES], made[h * half : (h + 1) * half, LANES:], ends], axis=0)
            for h in range(2)
        ]
        first = core == 0
        kept[p] = jnp.where(first, parts[0], parts[1])
        sent[p] = jnp.where(first, parts[1], parts[0])

    def project_four(i, carry):
        for n in range(4):
            project(4 * i + n)
        return carry

    lax.fori_loop(0, panels // 4, project_four, 0)


def update_body(arrived, chosen, sent):
    total = arrived[0]
    for n in range(1, arrived.shape[0]):
        total = total + arrived[n]
    p = lax.axis_index("row") // 2
    core = lax.axis_index("row") % 2
    half = (total.shape[0] - 8) // 2
    first = core * half
    lam = joined(chosen, p)
    right = column_of(lam)
    right = jnp.where(core == 0, right[:half], right[half : 2 * half])
    line = lax.broadcasted_iota(jnp.int32, (half, LANES), 0) + first
    lane = lax.broadcasted_iota(jnp.int32, (half, LANES), 1)
    same = line == lane
    spacing = right - lam[:, :LANES] + same.astype(F32)
    gram = total[2 * half : 2 * half + 1]
    numerator = total[:half]
    low = jnp.where(same, 1.0 + 0.5 * (1.0 - gram), numerator / spacing)
    high = total[half : 2 * half] / (right - lam[:, LANES:])
    roots = jnp.where(same, numerator / jnp.where(same, gram, 1.0) + right, 0.0)
    ends = jnp.broadcast_to(jnp.sum(roots, axis=0, keepdims=True), (8, LANES))
    made = jnp.concatenate([low, high, ends], axis=0)
    for n in range(sent.shape[0]):
        sent[n] = made


def refine_body(mine, other, formed, updated, sums, roots):
    panels, size = formed.shape[:2]
    own = size // 4
    half = own // 2
    zero = lax.axis_index("row") % 2 == 0

    def panel(p):
        a, b = mine[p], other[p]
        low = jnp.where(zero, a, b)
        high = jnp.where(zero, b, a)
        u = jnp.concatenate(
            [
                jnp.concatenate([low[:half], low[half:own]], axis=1),
                jnp.concatenate([high[:half], high[half:own]], axis=1),
            ],
            axis=0,
        )
        made = dot(jnp.concatenate(split(u), axis=0), formed[p], NN)
        made = made[:own] + made[own:]
        updated[p] = made
        total = jnp.zeros((own, LANES), F32)
        for k in range(made.shape[1] // LANES):
            piece = made[:, k * LANES : (k + 1) * LANES]
            total = total + piece * piece
        sums[pl.ds(p, 1), :] = row_of(jnp.concatenate([total, jnp.zeros_like(total)], axis=0))
        roots[pl.ds(p, 1), :] = low[own : own + 1] + high[own : own + 1]

    def four(i, carry):
        for n in range(4):
            panel(4 * i + n)
        return carry

    lax.fori_loop(0, panels // 4, four, 0)


def scale_body(sums_a, sums_b, sums_c, sums_d, updated, refined, sums, scaled, sems, *, order):
    panels, own, rows = updated.shape
    sums[...] = sums_a[...] + sums_b[...] + sums_c[...] + sums_d[...]

    def copy(p):
        return pltpu.make_async_copy(scaled.at[p], refined.at[p], sems.at[p])

    def panel(p, carry):
        factor = column_of(jnp.sqrt(order / sums[pl.ds(p, 1), :]))[:own]
        for k in range(rows // LANES):
            lanes = slice(k * LANES, (k + 1) * LANES)
            scaled[p, :, lanes] = updated[p, :, lanes] * factor
        copy(p).start()
        return carry

    def wait(p, carry):
        copy(p).wait()
        return carry

    lax.fori_loop(0, panels, panel, 0)
    lax.fori_loop(0, panels, wait, 0)


def vmem():
    return pl.BlockSpec(memory_space=pltpu.VMEM)


def hbm():
    return pl.BlockSpec(memory_space=pltpu.HBM)


def anywhere():
    return pl.BlockSpec(memory_space=pl.ANY)


def shards(
    pole_values, rank_one, deflated, onsite_energy, secular_roots, column_order,
    q_blocks, diag_blocks, coupling_blocks,
):
    rows = pole_values.shape[0]
    panels, size = secular_roots.shape
    count, block, _ = q_blocks.shape
    own = size // lax.axis_size("col")
    row_count = lax.axis_size("row")
    chips = row_count // 2
    forward = [(i, (i + 1) % row_count) for i in range(row_count)]
    backward = [(i, (i - 1) % row_count) for i in range(row_count)]
    weights = rank_one * (1 - deflated).astype(F32)
    pair = jnp.stack([pole_values, weights])
    before = lax.ppermute(q_blocks[count - 1], "row", forward)
    after = lax.ppermute(
        jnp.concatenate([q_blocks[0], coupling_blocks[0].astype(BF16)], axis=0), "row", backward
    )
    pair_before = lax.ppermute(pair[:, rows - block :], "row", forward)
    pair_after = lax.ppermute(pair[:, :block], "row", backward)
    vectors = (pole_values[None], rank_one[None], deflated[None])

    chosen, squares = pl.pallas_call(
        squares_body,
        out_shape=[
            pltpu.VMEM((2 * panels, LANES), F32),
            pltpu.VMEM((2 * panels, LANES), F32),
        ],
        in_specs=[hbm()] * 5,
        out_specs=[vmem()] * 2,
        scratch_shapes=[
            pltpu.VMEM((panels, size), F32),
            pltpu.VMEM((panels, size), jnp.int32),
            pltpu.VMEM((1, rows), F32),
            pltpu.VMEM((1, rows), F32),
            pltpu.VMEM((1, rows), jnp.int32),
            pltpu.VMEM((1, rows), F32),
            pltpu.VMEM((2, size, LANES), F32),
            pltpu.SemaphoreType.DMA((5,)),
        ],
        compiler_params=pltpu.CompilerParams(vmem_limit_bytes=8 * MIB),
        name="squares",
    )(secular_roots, column_order, *vectors)

    depth = own + 8
    formed, kept, sent = pl.pallas_call(
        form_body,
        out_shape=[
            pltpu.VMEM((panels, size, rows), BF16),
            pltpu.VMEM((panels, depth, LANES), F32),
            pltpu.VMEM((panels, depth, LANES), F32),
        ],
        in_specs=[vmem()] * 5 + [hbm()] * 4 + [vmem()] * 2 + [hbm()] + [anywhere()] * 2 + [hbm()] * 2,
        out_specs=[vmem()] * 3,
        scratch_shapes=[
            pltpu.VMEM((2, size, rows), BF16),
            pltpu.VMEM((2, panels * own, block), BF16),
            pltpu.VMEM((panels, 2 * own, rows), BF16),
            pltpu.VMEM((2, panels * own, block), F32),
            pltpu.VMEM((2, size, LANES), F32),
            pltpu.VMEM((panels, own, LANES), F32),
            pltpu.VMEM((2, size, LANES), F32),
            pltpu.VMEM((2 * panels, LANES), F32),
            pltpu.VMEM((count, block, block), F32),
            pltpu.VMEM((count, block, block), F32),
            pltpu.VMEM((count, block, block), BF16),
            pltpu.VMEM((block, block), BF16),
            pltpu.VMEM((2 * block, block), BF16),
            pltpu.VMEM((2, 2, block, block), BF16),
            pltpu.VMEM((count, 2, block, block), BF16),
            pltpu.VMEM((1, rows), F32),
            pltpu.VMEM((1, rows), F32),
            pltpu.VMEM((1, rows), jnp.int32),
            pltpu.VMEM((1, rows), F32),
            pltpu.VMEM((1, rows), F32),
            pltpu.VMEM((panels * own, LANES), F32),
            pltpu.SemaphoreType.DMA((9,)),
        ],
        compiler_params=pltpu.CompilerParams(vmem_limit_bytes=38 * MIB),
        name="form",
    )(
        chosen, *over_rows(squares), *vectors, onsite_energy[None], pair_before, pair_after,
        q_blocks, before, after, diag_blocks, coupling_blocks,
    )

    swap = [(i, i ^ 1) for i in range(row_count)]
    groups = [[c + 2 * k for k in range(chips)] for c in range(2)]
    spread = functools.partial(
        lax.all_to_all, axis_name="row", split_axis=0, concat_axis=0, tiled=True, axis_index_groups=groups
    )
    arrived = spread(kept + lax.ppermute(sent, "row", swap))
    shares = pl.pallas_call(
        update_body,
        out_shape=jax.ShapeDtypeStruct((chips, depth, LANES), F32),
        in_specs=[vmem()] * 2,
        out_specs=vmem(),
        compiler_params=pltpu.CompilerParams(vmem_limit_bytes=8 * MIB),
        name="update",
    )(arrived, chosen)
    mine = spread(shares)
    other = lax.ppermute(mine, "row", swap)

    updated, sums, roots = pl.pallas_call(
        refine_body,
        out_shape=[
            pltpu.VMEM((panels, own, rows), F32),
            pltpu.VMEM((panels, LANES), F32),
            jax.ShapeDtypeStruct((panels, LANES), F32),
        ],
        in_specs=[vmem()] * 3,
        out_specs=[vmem()] * 3,
        compiler_params=pltpu.CompilerParams(vmem_limit_bytes=12 * MIB),
        name="refine",
    )(mine, other, formed)
    refined = pl.pallas_call(
        functools.partial(scale_body, order=float(rows * row_count)),
        out_shape=jax.ShapeDtypeStruct((panels, own, rows), F32),
        in_specs=[vmem()] * 5,
        out_specs=hbm(),
        scratch_shapes=[
            pltpu.VMEM((panels, LANES), F32),
            pltpu.VMEM((panels, own, rows), F32),
            pltpu.SemaphoreType.DMA((panels,)),
        ],
        compiler_params=pltpu.CompilerParams(vmem_limit_bytes=12 * MIB),
        name="scale",
    )(*over_rows(sums), updated)
    return jnp.transpose(refined, (0, 2, 1)), roots[:, :own]


def over_rows(value):
    def to(step):
        return [(i, step(i // 8, i // 2 % 4, i % 2)) for i in range(32)]

    value = value + lax.ppermute(value, "row", to(lambda z, x, c: z * 8 + x * 2 + 1 - c))
    along_x = [to(lambda z, x, c, k=k: z * 8 + (x + k) % 4 * 2 + c) for k in (1, 2, 3)]
    value = value + sum([lax.ppermute(value, "row", move) for move in along_x])
    along_z = [to(lambda z, x, c, k=k: (z + k) % 4 * 8 + x * 2 + c) for k in (1, 2, 3)]
    return [value] + [lax.ppermute(value, "row", move) for move in along_z]


def solution(mesh):
    placed = (
        P("row"), P("row"), P("row"), P("row"), P(), P(),
        P("row", None, None), P("row", None, None), P("row", None, None),
    )
    return jax.shard_map(
        shards,
        mesh=mesh,
        in_specs=placed,
        out_specs=(P(None, "row", "col"), P(None, "col")),
        check_vma=False,
    )
```
